32 devices in a mesh: sens: 4 (over y, x), par: 8 (over z, core).
Axes of the slice: x: 2, y: 2, z: 4, core: 2. Of those that a mesh axis runs over, the one named last changes fastest.
Arguments:
- kernel: bfloat16 [2, 129, 64, 8192], P(None, None, 'sens', 'par'), may hold values from -0.0625 to 0.0625
- param: float32 [128, 2, 8192], P(None, None, 'par'), may hold values from -6 to 6
- observed: float32 [64, 128], P('sens'), may hold values from -6 to 6
- noise_scale: float32 [64], P('sens'), may hold values from 0.3 to 3
- robust_flags: int32 [64, 128], P('sens'), may hold values 0 or 1
- kappa_field: float32 [8192], P('par'), may hold values from 0.01 to 0.1
- coupling: float32 [8192], P('par'), may hold values from 0.05 to 0.2
- neighbours: int32 [8, 4], replicated, may hold values from -1 to 7, as said below
Outputs:
- gradient: float32 [128, 2, 8192], P(None, None, 'par')
- direction: float32 [128, 2, 8192], P(None, None, 'par')
The draws below stay inside these ranges and needn't reach their ends.
Inputs may be any that keep to these rules, and one draw needn't show every extreme that they name: `neighbours`: row k lists the tiles west, east, south and north of tile k, or -1 where there is none; the tiles fill a grid of 2 columns and 4 rows in an order drawn from the seed, and the relations are mutual.
All inputs are finite; a program needn't handle non-finite values. No bound on the sum of `robust_flags` on one device may be relied on, other than what follows from the above.
Results may differ from the reference program's by a relative error of at most 0.003.
Values may be sent and summed in bfloat16 or wider, within the bound.
A program may use at most 128 MiB of HBM per device.

```python
import math
import jax
import jax.numpy as jnp
from jax import lax

NT = 128
NSAMP = 2
SWEEPS = 8
TSIDE = 32
NF = 129
C_DEV = 1024
NTILES = 8
NC = 8192
NS = 64


def draw_neighbours(key, part):
    tile_count = NTILES
    columns = tile_count // 4
    position = jax.random.permutation(key, tile_count).astype(jnp.int32)
    tile_at = jnp.zeros((tile_count,), jnp.int32).at[position].set(jnp.arange(tile_count, dtype=jnp.int32))
    column_of = position % columns
    row_of = position // columns

    def lookup(inside, target):
        return jnp.where(inside, tile_at[jnp.clip(target, 0, tile_count - 1)], -1)
    west_tile = lookup(column_of > 0, position - 1)
    east_tile = lookup(column_of < columns - 1, position + 1)
    south_tile = lookup(row_of > 0, position - columns)
    north_tile = lookup(row_of < 3, position + columns)
    return jnp.stack([west_tile, east_tile, south_tile, north_tile], 1).astype(jnp.int32)


def place_ends(array, stream_key, smallest, high):
    spot = [jax.random.randint(jax.random.fold_in(stream_key, axis), (), 0, length) for axis, length in enumerate(array.shape)]
    widest = array.shape.index(max(array.shape))
    neighbour = spot[:widest] + [(spot[widest] + 1) % array.shape[widest]] + spot[widest + 1:]
    return array.at[tuple(spot)].set(smallest).at[tuple(neighbour)].set(high)


def block_scale(own_key, dims, pieces, low, top_value):
    level, own = 1.0, jax.random.fold_in(own_key, 6)
    for dim, blocks in pieces:
        steps = jnp.exp(jax.random.uniform(jax.random.fold_in(own, dim), (blocks,), jnp.float32, low / len(pieces), top_value / len(pieces)))
        level = level * jnp.repeat(steps, dims[dim] // blocks).reshape([-1 if axis == dim else 1 for axis in range(len(dims))])
    return level


def noise(rng, extent, width, most, pieces=(), kind=jnp.bfloat16):
    factor_of = block_scale(rng, extent, pieces, -0.22, 0.18) if pieces else 1.0
    drawn = jax.random.normal(rng, extent, jnp.float32) * width * factor_of
    return jnp.minimum(jnp.maximum(drawn, -most), most).astype(kind)


def setup_inputs(seed: int = 0) -> dict:
    arg_keys = jax.random.split(jax.random.key(seed), 9)
    return {
        "kernel": noise(arg_keys[0], (2, NF, NS, NC), NC ** -0.5, 0.0625, ((2, 4), (3, 8))),
        "param": noise(arg_keys[1], (NT, NSAMP, NC), 1.0, 6.0, ((2, 8),), jnp.float32),
        "observed": noise(arg_keys[2], (NS, NT), 1.0, 6.0, ((0, 4),), jnp.float32),
        "noise_scale": jnp.clip(jnp.exp(math.log(3.0) - 2.3025851 * jax.random.uniform(arg_keys[3], (NS,), jnp.float32) ** block_scale(arg_keys[3], (NS,), ((0, 4),), -0.2, 0.2)), 0.3, 3.0),
        "robust_flags": place_ends((jax.random.randint(arg_keys[4], (NS, NT), 0, 2) < 1).astype(jnp.int32), jax.random.fold_in(arg_keys[4], 1), 0, 1),
        "kappa_field": jnp.clip(jnp.exp(math.log(0.1) - 2.3025851 * jax.random.uniform(arg_keys[5], (NC,), jnp.float32) ** block_scale(arg_keys[5], (NC,), ((0, 8),), -0.2, 0.2)), 0.01, 0.1),
        "coupling": jnp.clip(jnp.exp(math.log(0.2) - 1.3862944 * jax.random.uniform(arg_keys[6], (NC,), jnp.float32) ** block_scale(arg_keys[6], (NC,), ((0, 8),), -0.2, 0.2)), 0.05, 0.2),
        "neighbours": draw_neighbours(jax.random.fold_in(arg_keys[8], 71), 0),
    }


huber_limit = 1.345


def tables(length):
    period = 2 * length
    frequency = jnp.arange(length + 1, dtype=jnp.int32)
    moment = jnp.arange(length, dtype=jnp.int32)
    phases = (frequency[:, None] * moment[None, :]) % period
    angles = phases.astype(jnp.float32) * (2.0 * jnp.pi / period)
    cosine = jnp.cos(angles)
    sines = jnp.sin(angles)
    forward = jnp.concatenate([cosine, -sines], 0)
    weight = jnp.where((frequency == 0) | (frequency == length), 1.0, 2.0).astype(jnp.float32) / period
    backward = jnp.concatenate([weight[:, None] * cosine, -weight[:, None] * sines], 0)
    return forward, backward


def residual_spectrum(predicted, observed, noise_scale, robust_flags, backward):
    length = observed.shape[1]
    sensor_count = predicted.shape[1]
    samples = predicted.shape[2]
    series = jnp.dot(backward.T, predicted.reshape(-1, sensor_count * samples), precision=lax.Precision.HIGHEST)
    series = series.reshape(length, sensor_count, samples)
    scaled = (series - observed.T[:, :, None]) / noise_scale[None, :, None]
    robust = jnp.where(robust_flags.T[:, :, None] == 1, jnp.clip(scaled, -huber_limit, huber_limit), scaled)
    weighted = robust / noise_scale[None, :, None]
    spectral = jnp.dot(backward, weighted.reshape(length, -1), precision=lax.Precision.HIGHEST)
    return spectral.reshape(-1, sensor_count, samples)


def neighbour_sum(values, neighbours):
    row_count, tile_count, cell_count = values.shape
    square = values.reshape(row_count, tile_count, TSIDE, TSIDE)
    edge_rows = jnp.stack([square[..., 0], square[..., -1], square[..., 0, :], square[..., -1, :]], 0)

    def facing(edge_index, column_index):
        target = neighbours[:, column_index]
        picked = jnp.take(edge_rows[edge_index], jnp.maximum(target, 0), axis=1)
        return jnp.where((target >= 0)[None, :, None], picked, 0.0)

    west_rim = facing(1, 0)
    east_rim = facing(0, 1)
    south_rim = facing(3, 2)
    north_rim = facing(2, 3)
    column = jnp.arange(cell_count) % TSIDE
    zeros_column = jnp.zeros_like(values[..., :1])
    east_side = jnp.where(column == TSIDE - 1, jnp.repeat(east_rim, TSIDE, axis=-1), jnp.concatenate([values[..., 1:], zeros_column], -1))
    west_side = jnp.where(column == 0, jnp.repeat(west_rim, TSIDE, axis=-1), jnp.concatenate([zeros_column, values[..., :-1]], -1))
    north_side = jnp.concatenate([values[..., TSIDE:], north_rim], -1)
    south_side = jnp.concatenate([south_rim, values[..., :-TSIDE]], -1)
    return east_side + west_side + north_side + south_side


def reference(kernel, param, observed, noise_scale, robust_flags, kappa_field, coupling, neighbours):
    length, samples, cell_total = param.shape
    forward, backward = tables(length)
    spectrum = jnp.dot(forward, param.reshape(length, -1), precision=lax.Precision.HIGHEST)
    spectrum = spectrum.reshape(2, length + 1, samples, cell_total).astype(jnp.bfloat16)

    def predict_one(frequency):
        block = kernel[:, frequency].astype(jnp.float32)
        source = spectrum[:, frequency].astype(jnp.float32)
        product = jnp.einsum('isc,jbc->ijsb', block, source)
        return product[0, 0] - product[1, 1], product[0, 1] + product[1, 0]

    cosine_part, sine_part = lax.map(predict_one, jnp.arange(length + 1))
    predicted = jnp.concatenate([cosine_part, sine_part], 0)
    adjoint = residual_spectrum(predicted, observed, noise_scale, robust_flags, backward).astype(jnp.bfloat16)
    adjoint = adjoint.reshape(2, length + 1, -1, samples)

    def adjoin_one(frequency):
        block = kernel[:, frequency].astype(jnp.float32)
        source = adjoint[:, frequency].astype(jnp.float32)
        product = jnp.einsum('isc,jsb->ijbc', block, source)
        return product[0, 0] + product[1, 1], product[0, 1] - product[1, 0]

    cosine_back, sine_back = lax.map(adjoin_one, jnp.arange(length + 1))
    summed = jnp.concatenate([cosine_back, sine_back], 0).reshape(2 * (length + 1), samples * cell_total)
    misfit = jnp.dot(forward.T, summed, precision=lax.Precision.HIGHEST)
    misfit = misfit.reshape(length * samples, NTILES, C_DEV)
    field_rows = param.reshape(length * samples, NTILES, C_DEV)
    diagonal = (kappa_field + 4.0 * coupling).reshape(NTILES, C_DEV)
    link = coupling.reshape(NTILES, C_DEV)
    gradient = misfit + diagonal * field_rows - link * neighbour_sum(field_rows, neighbours)
    direction = jnp.zeros_like(gradient)
    for sweep in range(SWEEPS):
        direction = (gradient + link * neighbour_sum(direction, neighbours)) / diagonal
    return gradient.reshape(length, samples, cell_total), direction.reshape(length, samples, cell_total)
```

```python
import functools

import jax
import jax.numpy as jnp
import numpy as np
from jax import lax
from jax.experimental import pallas as pl
from jax.experimental.pallas import tpu as pltpu
from jax.sharding import PartitionSpec as P

SWEEPS = 8
TSIDE = 32
LANES = 128
GROUP = 16
HALF = 8
WIDE = 256

huber_limit = 1.345

MESH = pl.DeviceIdType.MESH
LAST = (((1,), (1,)), ((), ()))
f32, bf16 = jnp.float32, jnp.bfloat16


def tables(length):
    period = 2 * length
    frequency = np.arange(length + 1)
    phases = frequency[:, None] * np.arange(length)[None, :] % period
    angles = phases * (2.0 * np.pi / period)
    cosine, sines = np.cos(angles), np.sin(angles)
    forward = np.stack([cosine, -sines], 0)
    weight = np.where((frequency == 0) | (frequency == length), 1.0, 2.0) / period
    return forward, forward * weight[:, None]


def halves(table):
    high = table.astype(np.float32).astype(jnp.bfloat16)
    low = (table - high.astype(np.float64)).astype(np.float32).astype(jnp.bfloat16)
    return high, low


def pairs(table):
    high, low = halves(table)
    return np.concatenate(
        [np.concatenate([high, high], 1), np.concatenate([low, np.zeros_like(low)], 1)], 0
    )


def all_tables(length):
    forward, backward = tables(length)
    count = length + 1
    groups = -(-count // GROUP)
    full = count // GROUP
    pad = ((0, 0), (0, groups * GROUP - count), (0, 0))

    def rows(table):
        table = np.pad(table, pad).reshape(2, groups, GROUP, length)
        return table.transpose(1, 0, 2, 3).reshape(groups * 2 * GROUP, length)

    fore, back = rows(forward), rows(backward)
    trans = np.pad(backward, pad).reshape(2, groups, 2, HALF, length)
    trans = trans.transpose(0, 2, 4, 1, 3).reshape(4 * length, groups * HALF)
    high, low = (part.T for part in halves(fore))
    cut = full * 2 * GROUP
    main, rest = slice(0, cut), slice(cut, None)
    misfit = np.concatenate(
        [high[:, main], high[:, main], low[:, main], high[:, rest], high[:, rest], low[:, rest]], 1
    )
    return pairs(fore), pairs(trans), pairs(back), misfit


def split(values):
    high = values.astype(bf16)
    return high, (values - high.astype(f32)).astype(bf16)


def split_wide(values):
    high = values.astype(bf16).astype(f32)
    return high, values - high


def remote(src, dst, send, recv, device):
    return pltpu.make_async_remote_copy(
        src_ref=src, dst_ref=dst, send_sem=send, recv_sem=recv, device_id=device, device_id_type=MESH
    )


def around(own, chunks, west, east, south, north):
    shape = own[0].shape
    lane = lax.broadcasted_iota(jnp.int32, shape, 1)
    column = lax.rem(lane, TSIDE)
    up = [pltpu.roll(v, LANES - TSIDE, 1) for v in own] + [north]
    down = [south] + [pltpu.roll(v, TSIDE, 1) for v in own]
    sums = []
    for j in range(chunks):
        east_side = jnp.where(column == TSIDE - 1, east(j), pltpu.roll(own[j], LANES - 1, 1))
        west_side = jnp.where(column == 0, west(j), pltpu.roll(own[j], 1, 1))
        north_side = jnp.where(lane < LANES - TSIDE, up[j], up[j + 1])
        south_side = jnp.where(lane >= TSIDE, down[j + 1], down[j])
        sums.append((east_side + west_side) + (north_side + south_side))
    return sums


def main_kernel(
    groups, tiles,
    kernel, param, observed, noise, flags, kappa, coupling, near, fore, trans, back, mist,
    grad_out, dir_out,
    blocks, halved, spectrum, packed, seen, bounded, wide, stacked, misfit, parts, landed, prior,
    rim, rims, kappas, couplings, grad, exact, grad_in, start, ratio, even, odd, dir_send, grad_all, dir_all,
    predicted, k_sem, k_send, k_recv, r_send, r_recv, c_send, c_recv, a_send, a_recv, e_send, e_recv,
    b_send, b_recv, d_send, d_recv, f_send, f_recv,
):
    sens, par = lax.axis_index("sens"), lax.axis_index("par")
    sensors, length = observed.shape
    freqs, pieces = spectrum.shape[0], blocks.shape[1]
    cells = halved.shape[2]
    samples = halved.shape[0]
    full = (length + 1) // GROUP
    chunks = cells // LANES
    columns = cells // WIDE
    stride = chunks * samples
    span = prior.shape[1]
    rows = span // tiles
    group_at = [lax.rem(sens + k, groups) for k in range(groups)]
    tile_at = [lax.rem(par + q, tiles) for q in range(tiles)]
    source_at = [lax.rem(par + tiles - q, tiles) for q in range(tiles)]

    barrier = pltpu.get_barrier_semaphore()
    for k in range(1, groups):
        pl.semaphore_signal(barrier, inc=1, device_id=(group_at[k], par), device_id_type=MESH)
    for q in range(1, tiles):
        pl.semaphore_signal(barrier, inc=1, device_id=(sens, tile_at[q]), device_id_type=MESH)

    loads = []
    for g in range(freqs):
        size = GROUP * sensors if g < full else (length + 1 - full * GROUP) * sensors
        for i in range(pieces):
            copy = pltpu.make_async_copy(
                kernel.at[i, pl.ds(g * GROUP * sensors, size)],
                blocks.at[g, i, pl.ds(0, size)],
                k_sem.at[g, i],
            )
            copy.start()
            loads.append(copy)

    for b in range(samples):
        for j in range(chunks):
            high, low = split(param[pl.ds(samples * j + b, length, stride=stride), :])
            at = slice(j * LANES, (j + 1) * LANES)
            halved[b, :length, at] = high
            halved[b, length:, at] = low

    half = freqs * 2 * GROUP
    for b in range(samples):
        for n in range(columns):
            at = slice(n * WIDE, (n + 1) * WIDE)
            both = jnp.dot(fore[...], halved[b, :, at], preferred_element_type=f32)
            rounded = (both[:half] + both[half:]).astype(bf16)
            for g in range(freqs):
                for k in range(2):
                    to, fro = (k * samples + b) * GROUP, (g * 2 + k) * GROUP
                    spectrum[g, to : to + GROUP, at] = rounded[fro : fro + GROUP]

    copies = LANES // sensors
    seen[...] = jnp.concatenate([observed[...]] * copies, 0).T
    bounded[...] = jnp.concatenate([flags[...].astype(f32)] * copies, 0).T
    deviation = jnp.concatenate([noise[...]] * copies, 1)
    inverse = 1.0 / deviation

    lanes64 = lax.broadcasted_iota(jnp.int32, (2 * samples * GROUP, WIDE), 1) // sensors
    rows64 = lax.rem(lax.broadcasted_iota(jnp.int32, (2 * samples * GROUP, WIDE), 0), GROUP)
    keep = lanes64 == rows64
    place = lax.broadcasted_iota(jnp.int32, (HALF, LANES), 1) // sensors
    side = samples * GROUP

    def pack(real, imag):
        total = jnp.concatenate([real[:side] - imag[side:], real[side:] + imag[:side]], 0)
        for step in range(copies.bit_length() - 1):
            total = total + pltpu.roll(total, sensors << step, 1)
        out = jnp.zeros((HALF, LANES), f32)
        for r in range(copies):
            out = jnp.where(place == r, total[r * HALF : (r + 1) * HALF], out)
        return out

    p_copies = []
    for g in range(freqs):
        for i in range(pieces):
            loads[g * pieces + i].wait()
        folded = []
        for i in range(pieces):
            if g < full:
                product = lax.dot_general(
                    spectrum[g], blocks[g, i], LAST, preferred_element_type=f32
                )
                product = jnp.where(keep, product, 0.0)
                folded.append(product[:, :LANES] + product[:, LANES:])
            else:
                product = lax.dot_general(
                    spectrum[g], blocks[g, i, :sensors], LAST, preferred_element_type=f32
                )
                filler = jnp.zeros((product.shape[0], LANES - sensors), f32)
                folded.append(jnp.concatenate([product, filler], 1))
        packed[g] = pack(*folded)
        if g == 0:
            pl.semaphore_wait(barrier, groups + tiles - 2)
        for q in range(1, tiles):
            copy = remote(
                packed.at[g], predicted.at[q - 1, g], k_send.at[g, q - 1], k_recv.at[g, q - 1],
                (sens, tile_at[q]),
            )
            copy.start()
            p_copies.append(copy)

    first = sens * span
    own_sample, own_time = first // length, lax.rem(first, length)
    own = [
        param[pl.ds(own_time * stride + samples * j + own_sample, span, stride=stride), :]
        for j in range(chunks)
    ]
    lane = lax.broadcasted_iota(jnp.int32, (span, LANES), 1)
    column = lax.rem(lane, TSIDE)
    quarter = lane // TSIDE
    edge = jnp.zeros((span, LANES), f32)
    for j in range(chunks):
        edge = jnp.where(column == j, pltpu.roll(own[j], j, 1) if j else own[j], edge)
        shift = (chunks + j - (TSIDE - 1)) % LANES
        edge = jnp.where(column == chunks + j, pltpu.roll(own[j], shift, 1), edge)
    upper = column >= TSIDE // 2
    edge = jnp.where(upper & (quarter == 0), pltpu.roll(own[0], 16, 1), edge)
    edge = jnp.where(upper & (quarter == 1), pltpu.roll(own[0], 32, 1), edge)
    edge = jnp.where(upper & (quarter == 2), pltpu.roll(own[-1], LANES - 16, 1), edge)
    edge = jnp.where(upper & (quarter == 3), own[-1], edge)
    rim[...] = edge.astype(bf16)
    c_copies = []
    for q in range(1, tiles):
        device = (sens, tile_at[q])
        c_copies.append(remote(rim, rims.at[par], r_send.at[q - 1], r_recv.at[q - 1], device))
        c_copies.append(
            remote(kappa, kappas.at[par], c_send.at[0, q - 1], c_recv.at[0, q - 1], device)
        )
        c_copies.append(
            remote(coupling, couplings.at[par], c_send.at[1, q - 1], c_recv.at[1, q - 1], device)
        )
    for copy in c_copies:
        copy.start()
    rims[tiles] = jnp.zeros((span, LANES), bf16)
    kappas[par] = kappa[...]
    couplings[par] = coupling[...]

    def beside(tile):
        return [jnp.where(near[s, tile] < 0, tiles, near[s, tile]) for s in range(4)]

    for copy in p_copies:
        copy.wait_recv()
    total = packed[...]
    for q in range(tiles - 1):
        total = total + predicted[q]
    high, low = split_wide(total.reshape(freqs * HALF, LANES))
    right = jnp.concatenate([high, low], 0).astype(bf16)
    both = jnp.dot(trans[...], right, preferred_element_type=f32)
    both = both[: 4 * length] + both[4 * length :]
    where = lax.broadcasted_iota(jnp.int32, (length, LANES), 1) // sensors
    sample_of, kind = lax.rem(where // 2, samples), where // (2 * samples) * 2 + lax.rem(where, 2)
    series = both[:length]
    for part in range(1, 4):
        series = jnp.where(kind == part, both[part * length : (part + 1) * length], series)
    adjoint = []
    for b in range(samples):
        mine = jnp.where(sample_of == b, series, 0.0)
        for step in range(copies.bit_length() - 1):
            mine = mine + pltpu.roll(mine, sensors << step, 1)
        scaled = (mine - seen[...]) * inverse
        robust = jnp.where(bounded[...] == 1.0, jnp.clip(scaled, -huber_limit, huber_limit), scaled)
        high, low = split(robust * inverse)
        both = jnp.dot(back[...], jnp.concatenate([high, low], 0), preferred_element_type=f32)
        adjoint.append(both[:half] + both[half:])
    own_row = lax.broadcasted_iota(jnp.int32, (HALF, LANES), 0)
    blank = jnp.zeros((HALF, LANES), f32)
    for g in range(freqs):
        for k in range(2):
            for b in range(samples):
                fro = (g * 2 + k) * GROUP
                piece = adjoint[b][fro : fro + GROUP]
                pick = [
                    jnp.where(own_row == place, piece[h * HALF : (h + 1) * HALF], 0.0)
                    for h in range(2)
                ]
                here = [
                    jnp.concatenate([pick[0], blank], 0), jnp.concatenate([blank, pick[1]], 0)
                ]
                to = (k * samples + b) * GROUP
                other = ((1 - k) * samples + b) * GROUP
                for h in range(2):
                    at = slice(h * LANES, (h + 1) * LANES)
                    wide[g, to : to + GROUP, at] = here[h].astype(bf16)
                    at = slice(WIDE + h * LANES, WIDE + (h + 1) * LANES)
                    turned = here[h] if k else -here[h]
                    wide[g, other : other + GROUP, at] = turned.astype(bf16)

    deep = full * 2 * GROUP
    a_copies = []
    for n in range(columns):
        at = slice(n * WIDE, (n + 1) * WIDE)
        for g in range(freqs):
            if g < full:
                product = jnp.dot(
                    wide[g], blocks[g, :, :, at].reshape(2 * WIDE, WIDE), preferred_element_type=f32
                )
            else:
                product = jnp.dot(
                    wide[g, :, :sensors], blocks[g, 0, :sensors, at], preferred_element_type=f32
                ) + jnp.dot(
                    wide[g, :, WIDE : WIDE + sensors], blocks[g, 1, :sensors, at],
                    preferred_element_type=f32,
                )
            high, low = split(product)
            for k in range(2):
                for b in range(samples):
                    fro = (k * samples + b) * GROUP
                    if g < full:
                        base, gap = (g * 2 + k) * GROUP, deep
                    else:
                        base, gap = 3 * deep + k * GROUP, 2 * GROUP
                    stacked[b, base : base + GROUP] = high[fro : fro + GROUP]
                    stacked[b, base + gap : base + gap + GROUP] = low[fro : fro + GROUP]
                    stacked[b, base + 2 * gap : base + 2 * gap + GROUP] = high[fro : fro + GROUP]
        for b in range(samples):
            result = jnp.dot(mist[...], stacked[b], preferred_element_type=f32)
            for piece in range(length // span):
                index = b * (length // span) + piece
                values = result[piece * span : (piece + 1) * span]
                misfit[n, index] = values
                parts[n, index] = values.astype(bf16)
        for k in range(1, groups):
            copy = remote(
                parts.at[n, group_at[k]], landed.at[k - 1, n], a_send.at[k - 1, n],
                a_recv.at[k - 1, n], (group_at[k], par),
            )
            copy.start()
            a_copies.append(copy)

    for copy in c_copies:
        copy.wait_recv()
    west_tile, east_tile, south_tile, north_tile = beside(par)
    west_rim, east_rim, south_rim, north_rim = (
        rims[index].astype(f32) for index in (west_tile, east_tile, south_tile, north_tile)
    )
    sums = around(
        own,
        chunks,
        lambda j: pltpu.roll(west_rim, LANES - chunks - j, 1),
        lambda j: pltpu.roll(east_rim, TSIDE - 1 - j, 1),
        jnp.where(lane < 16, pltpu.roll(south_rim, 48, 1), pltpu.roll(south_rim, 32, 1)),
        jnp.where(lane >= LANES - 16, pltpu.roll(north_rim, 64, 1), pltpu.roll(north_rim, 80, 1)),
    )
    for j in range(chunks):
        strength = coupling[:, j * LANES : (j + 1) * LANES]
        diagonal = kappa[:, j * LANES : (j + 1) * LANES] + 4.0 * strength
        at = slice(j * LANES % WIDE, j * LANES % WIDE + LANES)
        prior[j * LANES // WIDE, :, at] = diagonal * own[j] - strength * sums[j]

    def prepare(tile, carry):
        strength = couplings[tile]
        rate = 1.0 / (kappas[tile] + 4.0 * strength)
        start[tile] = jnp.broadcast_to(rate, (rows, cells))
        ratio[tile] = jnp.broadcast_to(strength * rate, (rows, cells))
        return carry

    lax.fori_loop(0, tiles, prepare, 0)
    even[tiles] = jnp.zeros((rows, cells), f32)
    odd[tiles] = jnp.zeros((rows, cells), f32)

    e_copies, b_copies = [], []
    for n in range(columns):
        total = misfit[n, sens] + prior[n]
        for k in range(1, groups):
            a_copies[n * (groups - 1) + k - 1].wait_recv()
            total = total + landed[k - 1, n].astype(f32)
        exact[n] = total.reshape(tiles, rows, WIDE)
        grad[n] = exact[n].astype(bf16)
        for q in range(1, tiles):
            copy = remote(
                exact.at[n, tile_at[q]], grad_in.at[par, n], b_send.at[n, q - 1],
                b_recv.at[n, q - 1], (sens, tile_at[q]),
            )
            copy.start()
            b_copies.append(copy)
        for k in range(1, groups):
            copy = remote(
                grad.at[n], grad_all.at[sens, n], e_send.at[n, k - 1], e_recv.at[n, k - 1],
                (group_at[k], par),
            )
            copy.start()
            e_copies.append(copy)
        grad_in[par, n] = exact[n, par]
        grad_all[sens, n] = grad[n]

    for copy in b_copies:
        copy.wait_recv()

    def begin(tile, carry):
        for n in range(columns):
            at = slice(n * WIDE, (n + 1) * WIDE)
            values = grad_in[tile, n] * start[tile, :, at]
            start[tile, :, at] = values
            even[tile, :, at] = values
        return carry

    lax.fori_loop(0, tiles, begin, 0)

    def relax(tile, old):
        west, east, south, north = beside(tile)

        def load(index, j):
            return old[index, :, j * LANES : (j + 1) * LANES]

        sums = around(
            [load(tile, j) for j in range(chunks)],
            chunks,
            lambda j: pltpu.roll(load(west, j), LANES - TSIDE + 1, 1),
            lambda j: pltpu.roll(load(east, j), TSIDE - 1, 1),
            pltpu.roll(load(south, chunks - 1), TSIDE, 1),
            pltpu.roll(load(north, 0), LANES - TSIDE, 1),
        )
        for j, total in enumerate(sums):
            at = slice(j * LANES, (j + 1) * LANES)
            yield at, start[tile, :, at] + ratio[tile, :, at] * total

    def sweep(count):
        old, new = (even, odd) if count % 2 == 0 else (odd, even)

        def one(tile, carry):
            for at, values in relax(tile, old):
                new[tile, :, at] = values
            return carry

        lax.fori_loop(0, tiles, one, 0, unroll=2)

    for count in range(SWEEPS - 2):
        sweep(count)
    last = even if SWEEPS % 2 == 0 else odd
    d_copies = []
    for q in list(range(1, tiles)) + [0]:
        for at, values in relax(tile_at[q], last):
            dir_send[tile_at[q], :, at] = values.astype(bf16)
        if q:
            copy = remote(
                dir_send.at[tile_at[q]], dir_all.at[sens, par], d_send.at[q - 1], d_recv.at[q - 1],
                (sens, tile_at[q]),
            )
            copy.start()
            d_copies.append(copy)
    dir_all[sens, par] = dir_send[par]
    f_copies = []
    for q in range(tiles):
        if q:
            d_copies[q - 1].wait_recv()
        piece = dir_all.at[sens, source_at[q]]
        for k in range(1, groups):
            copy = remote(
                piece, piece, f_send.at[k - 1, q], f_recv.at[k - 1, q], (group_at[k], par)
            )
            copy.start()
            f_copies.append(copy)

    def place_at(index, j):
        first = index * rows
        sample, time = first // length, lax.rem(first, length)
        return pl.ds(time * stride + samples * j + sample, rows, stride=stride)

    for copy in e_copies:
        copy.wait_recv()

    def unpack_grad(index, carry):
        group, block = index // tiles, lax.rem(index, tiles)
        for j in range(chunks):
            at = slice(j * LANES % WIDE, j * LANES % WIDE + LANES)
            grad_out[place_at(index, j), :] = grad_all[
                group, j * LANES // WIDE, block, :, at
            ].astype(f32)
        return carry

    lax.fori_loop(0, groups * tiles, unpack_grad, 0)
    for copy in f_copies:
        copy.wait_recv()

    def unpack_dir(index, carry):
        group, block = index // tiles, lax.rem(index, tiles)
        for j in range(chunks):
            at = slice(j * LANES, (j + 1) * LANES)
            dir_out[place_at(index, j), :] = dir_all[group, block, :, at].astype(f32)
        return carry

    lax.fori_loop(0, groups * tiles, unpack_dir, 0)
    for copy in p_copies + c_copies + a_copies + e_copies + b_copies + d_copies + f_copies:
        copy.wait_send()


def per_device(
    kernel, param, observed, noise_scale, robust_flags, kappa_field, coupling, neighbours
):
    length, samples, cells = param.shape
    parts, count, sensors = kernel.shape[:3]
    groups, tiles = lax.axis_size("sens"), lax.axis_size("par")
    chunks, columns = cells // LANES, cells // WIDE
    freqs = -(-count // GROUP)
    span = length * samples // groups
    rows = span // tiles
    block = (rows, cells)
    raw = param.reshape(length, samples, chunks, LANES).transpose(0, 2, 1, 3)
    raw = raw.reshape(length * chunks * samples, LANES)
    consts = all_tables(length)
    vmem, smem = pl.BlockSpec(memory_space=pltpu.VMEM), pl.BlockSpec(memory_space=pltpu.SMEM)
    dma, scratch = pltpu.SemaphoreType.DMA, pltpu.VMEM
    out = jax.ShapeDtypeStruct(raw.shape, f32)
    sems = [
        (freqs, tiles - 1), (tiles - 1,), (2, tiles - 1), (groups - 1, columns),
        (columns, groups - 1), (columns, tiles - 1), (tiles - 1,), (groups - 1, tiles),
    ]
    gradient, direction = pl.pallas_call(
        functools.partial(main_kernel, groups, tiles),
        out_shape=(out, out),
        in_specs=[pl.BlockSpec(memory_space=pl.ANY)] + [vmem] * 6 + [smem] + [vmem] * 4,
        out_specs=(vmem, vmem),
        scratch_shapes=[
            scratch((freqs, parts, GROUP * sensors, cells), bf16),
            scratch((samples, 2 * length, cells), bf16),
            scratch((freqs, 2 * samples * GROUP, cells), bf16),
            scratch((freqs, HALF, LANES), f32),
            scratch((length, LANES), f32),
            scratch((length, LANES), f32),
            scratch((freqs, 2 * samples * GROUP, 2 * WIDE), bf16),
            scratch((samples, 3 * freqs * 2 * GROUP, WIDE), bf16),
            scratch((columns, groups, span, WIDE), f32),
            scratch((columns, groups, span, WIDE), bf16),
            scratch((groups - 1, columns, span, WIDE), bf16),
            scratch((columns, span, WIDE), f32),
            scratch((span, LANES), bf16),
            scratch((tiles + 1, span, LANES), bf16),
            scratch((tiles, 1, cells), f32),
            scratch((tiles, 1, cells), f32),
            scratch((columns, tiles, rows, WIDE), bf16),
            scratch((columns, tiles, rows, WIDE), f32),
            scratch((tiles, columns, rows, WIDE), f32),
            scratch((tiles,) + block, f32),
            scratch((tiles,) + block, f32),
            scratch((tiles + 1,) + block, f32),
            scratch((tiles + 1,) + block, f32),
            scratch((tiles,) + block, bf16),
            scratch((groups, columns, tiles, rows, WIDE), bf16),
            scratch((groups, tiles) + block, bf16),
            scratch((tiles - 1, freqs, HALF, LANES), f32),
            dma((freqs, parts)),
        ]
        + [dma(shape) for shape in sems for _ in range(2)],
        compiler_params=pltpu.CompilerParams(collective_id=0, has_side_effects=True),
    )(
        kernel.reshape(parts, count * sensors, cells), raw, observed, noise_scale[None],
        robust_flags, kappa_field[None], coupling[None], neighbours.T, *consts,
    )

    def restore(values):
        values = values.reshape(length, chunks, samples, LANES).transpose(0, 2, 1, 3)
        return values.reshape(param.shape)

    return restore(gradient), restore(direction)


def solution(mesh):
    return jax.shard_map(
        per_device,
        mesh=mesh,
        in_specs=(
            P(None, None, "sens", "par"),
            P(None, None, "par"),
            P("sens", None),
            P("sens"),
            P("sens", None),
            P("par"),
            P("par"),
            P(),
        ),
        out_specs=(P(None, None, "par"), P(None, None, "par")),
        check_vma=False,
    )
```

```python
import functools

import jax
import jax.numpy as jnp
import numpy as np
from jax import lax
from jax.experimental import pallas as pl
from jax.experimental.pallas import tpu as pltpu
from jax.sharding import PartitionSpec as P

SWEEPS = 8
TSIDE = 32
LANES = 128
GROUP = 16
HALF = 8
WIDE = 256

huber_limit = 1.345

MESH = pl.DeviceIdType.MESH
LAST = (((1,), (1,)), ((), ()))
f32, bf16 = jnp.float32, jnp.bfloat16


def tables(length):
    period = 2 * length
    frequency = np.arange(length + 1)
    phases = frequency[:, None] * np.arange(length)[None, :] % period
    angles = phases * (2.0 * np.pi / period)
    cosine, sines = np.cos(angles), np.sin(angles)
    forward = np.stack([cosine, -sines], 0)
    weight = np.where((frequency == 0) | (frequency == length), 1.0, 2.0) / period
    return forward, forward * weight[:, None]


def halves(table):
    high = table.astype(np.float32).astype(jnp.bfloat16)
    low = (table - high.astype(np.float64)).astype(np.float32).astype(jnp.bfloat16)
    return high, low


def pairs(table):
    high, low = halves(table)
    return np.concatenate(
        [np.concatenate([high, high], 1), np.concatenate([low, np.zeros_like(low)], 1)], 0
    )


def all_tables(length):
    forward, backward = tables(length)
    count = length + 1
    groups = -(-count // GROUP)
    full = count // GROUP
    pad = ((0, 0), (0, groups * GROUP - count), (0, 0))

    def rows(table):
        table = np.pad(table, pad).reshape(2, groups, GROUP, length)
        return table.transpose(1, 0, 2, 3).reshape(groups * 2 * GROUP, length)

    fore, back = rows(forward), rows(backward)
    trans = np.pad(backward, pad).reshape(2, groups, 2, HALF, length)
    trans = trans.transpose(0, 2, 4, 1, 3).reshape(4 * length, groups * HALF)
    high, low = (part.T for part in halves(fore))
    cut = full * 2 * GROUP
    main, rest = slice(0, cut), slice(cut, None)
    misfit = np.concatenate(
        [high[:, main], high[:, main], low[:, main], high[:, rest], high[:, rest], low[:, rest]], 1
    )
    return pairs(fore), pairs(trans), pairs(back), misfit


def split(values):
    high = values.astype(bf16)
    return high, (values - high.astype(f32)).astype(bf16)


def split_wide(values):
    high = values.astype(bf16).astype(f32)
    return high, values - high


def remote(src, dst, send, recv, device):
    return pltpu.make_async_remote_copy(
        src_ref=src, dst_ref=dst, send_sem=send, recv_sem=recv, device_id=device, device_id_type=MESH
    )


def around(own, chunks, west, east, south, north):
    shape = own[0].shape
    lane = lax.broadcasted_iota(jnp.int32, shape, 1)
    column = lax.rem(lane, TSIDE)
    up = [pltpu.roll(v, LANES - TSIDE, 1) for v in own] + [north]
    down = [south] + [pltpu.roll(v, TSIDE, 1) for v in own]
    sums = []
    for j in range(chunks):
        east_side = jnp.where(column == TSIDE - 1, east(j), pltpu.roll(own[j], LANES - 1, 1))
        west_side = jnp.where(column == 0, west(j), pltpu.roll(own[j], 1, 1))
        north_side = jnp.where(lane < LANES - TSIDE, up[j], up[j + 1])
        south_side = jnp.where(lane >= TSIDE, down[j + 1], down[j])
        sums.append((east_side + west_side) + (north_side + south_side))
    return sums


def main_kernel(
    groups, tiles,
    kernel, param_in, fore_in, trans_in, back_in, mist_in, observed, noise, flags, kappa, coupling, near,
    grad_all, dir_all,
    param, fore, trans, back, mist, blocks, halved, spectrum, packed, seen, bounded, wide, stacked,
    misfit, parts, landed, prior, rim, rims, kappas, couplings, grad, exact, grad_in, start, ratio,
    even, odd, dir_send, mine_out, others, k_sem, l_sem, k_send, k_recv, r_send, r_recv, c_send, c_recv,
    a_send, a_recv, e_send, e_recv, b_send, b_recv, d_send, d_recv, f_send, f_recv,
):
    sens, par = lax.axis_index("sens"), lax.axis_index("par")
    sensors, length = observed.shape
    freqs, pieces = spectrum.shape[0], blocks.shape[1]
    cells = halved.shape[2]
    samples = halved.shape[0]
    full = (length + 1) // GROUP
    chunks = cells // LANES
    columns = cells // WIDE
    stride = chunks * samples
    span = prior.shape[1]
    rows = span // tiles
    group_at = [lax.rem(sens + k, groups) for k in range(groups)]
    tile_at = [lax.rem(par + q, tiles) for q in range(tiles)]
    source_at = [lax.rem(par + tiles - q, tiles) for q in range(tiles)]

    barrier = pltpu.get_barrier_semaphore()
    for k in range(1, groups):
        pl.semaphore_signal(barrier, inc=1, device_id=(group_at[k], par), device_id_type=MESH)
    for q in range(1, tiles):
        pl.semaphore_signal(barrier, inc=1, device_id=(sens, tile_at[q]), device_id_type=MESH)

    early = [
        pltpu.make_async_copy(source, target, l_sem.at[index])
        for index, (source, target) in enumerate(
            [(param_in, param), (fore_in, fore), (trans_in, trans), (back_in, back), (mist_in, mist)]
        )
    ]

    def fetch(g, i, size):
        return pltpu.make_async_copy(
            kernel.at[i, pl.ds(g * GROUP * sensors, size)],
            blocks.at[g, i, pl.ds(0, size)],
            k_sem.at[g, i],
        )

    whole, rest = GROUP * sensors, (length + 1 - full * GROUP) * sensors
    for copy in early[:2]:
        copy.start()

    def begin_fetch(g, carry):
        for i in range(pieces):
            fetch(g, i, whole).start()
        return carry

    lax.fori_loop(0, full, begin_fetch, 0)
    for i in range(pieces):
        fetch(full, i, rest).start()
    for copy in early[2:]:
        copy.start()

    copies = LANES // sensors
    seen[...] = jnp.concatenate([observed[...]] * copies, 0).T
    bounded[...] = jnp.concatenate([flags[...].astype(f32)] * copies, 0).T
    deviation = jnp.concatenate([noise[...]] * copies, 1)
    inverse = 1.0 / deviation

    for copy in early[:2]:
        copy.wait()
    for b in range(samples):
        for j in range(chunks):
            high, low = split(param[pl.ds(samples * j + b, length, stride=stride), :])
            at = slice(j * LANES, (j + 1) * LANES)
            halved[b, :length, at] = high
            halved[b, length:, at] = low

    half = freqs * 2 * GROUP
    for b in range(samples):
        for n in range(columns):
            at = slice(n * WIDE, (n + 1) * WIDE)
            both = jnp.dot(fore[...], halved[b, :, at], preferred_element_type=f32)
            rounded = (both[:half] + both[half:]).astype(bf16)
            for g in range(freqs):
                for k in range(2):
                    to, fro = (k * samples + b) * GROUP, (g * 2 + k) * GROUP
                    spectrum[g, to : to + GROUP, at] = rounded[fro : fro + GROUP]

    lanes64 = lax.broadcasted_iota(jnp.int32, (2 * samples * GROUP, WIDE), 1) // sensors
    rows64 = lax.rem(lax.broadcasted_iota(jnp.int32, (2 * samples * GROUP, WIDE), 0), GROUP)
    keep = lanes64 == rows64
    place = lax.broadcasted_iota(jnp.int32, (HALF, LANES), 1) // sensors
    side = samples * GROUP

    def pack(real, imag):
        total = jnp.concatenate([real[:side] - imag[side:], real[side:] + imag[:side]], 0)
        for step in range(copies.bit_length() - 1):
            total = total + pltpu.roll(total, sensors << step, 1)
        out = jnp.zeros((HALF, LANES), f32)
        for r in range(copies):
            out = jnp.where(place == r, total[r * HALF : (r + 1) * HALF], out)
        return out

    for g in range(freqs):
        size = whole if g < full else rest
        for i in range(pieces):
            fetch(g, i, size).wait()
        folded = []
        for i in range(pieces):
            product = lax.dot_general(
                spectrum[g], blocks[g, i, :size], LAST, preferred_element_type=f32
            )
            if g < full:
                product = jnp.where(keep, product, 0.0)
                folded.append(product[:, :LANES] + product[:, LANES:])
            else:
                filler = jnp.zeros((product.shape[0], LANES - sensors), f32)
                folded.append(jnp.concatenate([product, filler], 1))
        packed[g] = pack(*folded)

    for copy in early[2:]:
        copy.wait()
    high, low = split_wide(packed[...].reshape(freqs * HALF, LANES))
    right = jnp.concatenate([high, low], 0).astype(bf16)
    both = jnp.dot(trans[...], right, preferred_element_type=f32)
    both = both[: 4 * length] + both[4 * length :]

    def lane_group(count):
        where = lax.broadcasted_iota(jnp.int32, (count, LANES), 1) // sensors
        kind = where // (2 * samples) * 2 + lax.rem(where, 2)
        return lax.rem(where // 2, samples), kind

    kind = lane_group(length)[1]
    series = both[:length]
    for part in range(1, 4):
        series = jnp.where(kind == part, both[part * length : (part + 1) * length], series)
    series = series + jnp.where(
        lax.rem(kind, 2) == 0, pltpu.roll(series, LANES - sensors, 1), pltpu.roll(series, sensors, 1)
    )
    series = series + pltpu.roll(series, LANES // 2, 1)
    short = length // 4
    sample_of, kind = lane_group(short)
    share = series[:short]
    for part in range(1, 4):
        share = jnp.where(kind == part, series[part * short : (part + 1) * short], share)
    mine_out[...] = share

    near_first = sorted(range(tiles), key=lambda q: min(q, tiles - q))
    far_first = near_first[:0:-1]
    pl.semaphore_wait(barrier, groups + tiles - 2)
    p_copies = []
    for q in far_first:
        copy = remote(
            mine_out, others.at[q - 1], k_send.at[q - 1], k_recv.at[q - 1], (sens, tile_at[q])
        )
        copy.start()
        p_copies.append(copy)

    first = sens * span
    own_sample, own_time = first // length, lax.rem(first, length)
    own = [
        param[pl.ds(own_time * stride + samples * j + own_sample, span, stride=stride), :]
        for j in range(chunks)
    ]
    lane = lax.broadcasted_iota(jnp.int32, (span, LANES), 1)
    column = lax.rem(lane, TSIDE)
    quarter = lane // TSIDE
    edge = jnp.zeros((span, LANES), f32)
    for j in range(chunks):
        edge = jnp.where(column == j, pltpu.roll(own[j], j, 1) if j else own[j], edge)
        shift = (chunks + j - (TSIDE - 1)) % LANES
        edge = jnp.where(column == chunks + j, pltpu.roll(own[j], shift, 1), edge)
    upper = column >= TSIDE // 2
    edge = jnp.where(upper & (quarter == 0), pltpu.roll(own[0], 16, 1), edge)
    edge = jnp.where(upper & (quarter == 1), pltpu.roll(own[0], 32, 1), edge)
    edge = jnp.where(upper & (quarter == 2), pltpu.roll(own[-1], LANES - 16, 1), edge)
    edge = jnp.where(upper & (quarter == 3), own[-1], edge)
    rim[...] = edge.astype(bf16)
    c_copies = []
    for q in range(1, tiles):
        device = (sens, tile_at[q])
        c_copies.append(remote(rim, rims.at[par], r_send.at[q - 1], r_recv.at[q - 1], device))
        c_copies.append(
            remote(kappa, kappas.at[par], c_send.at[0, q - 1], c_recv.at[0, q - 1], device)
        )
        c_copies.append(
            remote(coupling, couplings.at[par], c_send.at[1, q - 1], c_recv.at[1, q - 1], device)
        )
    for copy in c_copies:
        copy.start()
    rims[tiles] = jnp.zeros((span, LANES), bf16)
    kappas[par] = kappa[...]
    couplings[par] = coupling[...]

    def beside(tile):
        return [jnp.where(near[s, tile] < 0, tiles, near[s, tile]) for s in range(4)]

    for copy in p_copies:
        copy.wait_recv()
    total = mine_out[...]
    for q in range(tiles - 1):
        total = total + others[q]
    adjoint = []
    for b in range(samples):
        mine = jnp.concatenate(
            [jnp.where((sample_of == b) & (kind == part), total, 0.0) for part in range(4)], 0
        )
        for step in range(copies.bit_length() - 1):
            mine = mine + pltpu.roll(mine, sensors << step, 1)
        scaled = (mine - seen[...]) * inverse
        robust = jnp.where(bounded[...] == 1.0, jnp.clip(scaled, -huber_limit, huber_limit), scaled)
        high, low = split(robust * inverse)
        both = jnp.dot(back[...], jnp.concatenate([high, low], 0), preferred_element_type=f32)
        adjoint.append(both[:half] + both[half:])
    own_row = lax.broadcasted_iota(jnp.int32, (HALF, LANES), 0)
    blank = jnp.zeros((HALF, LANES), f32)
    for g in range(freqs):
        for k in range(2):
            for b in range(samples):
                fro = (g * 2 + k) * GROUP
                piece = adjoint[b][fro : fro + GROUP]
                pick = [
                    jnp.where(own_row == place, piece[h * HALF : (h + 1) * HALF], 0.0)
                    for h in range(2)
                ]
                here = [
                    jnp.concatenate([pick[0], blank], 0), jnp.concatenate([blank, pick[1]], 0)
                ]
                to = (k * samples + b) * GROUP
                other = ((1 - k) * samples + b) * GROUP
                for h in range(2):
                    at = slice(h * LANES, (h + 1) * LANES)
                    wide[g, to : to + GROUP, at] = here[h].astype(bf16)
                    at = slice(WIDE + h * LANES, WIDE + (h + 1) * LANES)
                    turned = here[h] if k else -here[h]
                    wide[g, other : other + GROUP, at] = turned.astype(bf16)

    deep = full * 2 * GROUP
    a_copies = []
    for n in range(columns):
        at = slice(n * WIDE, (n + 1) * WIDE)
        for g in range(freqs):
            if g < full:
                product = jnp.dot(
                    wide[g], blocks[g, :, :, at].reshape(2 * WIDE, WIDE), preferred_element_type=f32
                )
            else:
                product = jnp.dot(
                    wide[g, :, :sensors], blocks[g, 0, :sensors, at], preferred_element_type=f32
                ) + jnp.dot(
                    wide[g, :, WIDE : WIDE + sensors], blocks[g, 1, :sensors, at],
                    preferred_element_type=f32,
                )
            high, low = split(product)
            for k in range(2):
                for b in range(samples):
                    fro = (k * samples + b) * GROUP
                    if g < full:
                        base, gap = (g * 2 + k) * GROUP, deep
                    else:
                        base, gap = 3 * deep + k * GROUP, 2 * GROUP
                    stacked[b, base : base + GROUP] = high[fro : fro + GROUP]
                    stacked[b, base + gap : base + gap + GROUP] = low[fro : fro + GROUP]
                    stacked[b, base + 2 * gap : base + 2 * gap + GROUP] = high[fro : fro + GROUP]
        for b in range(samples):
            result = jnp.dot(mist[...], stacked[b], preferred_element_type=f32)
            for piece in range(length // span):
                index = b * (length // span) + piece
                values = result[piece * span : (piece + 1) * span]
                misfit[n, index] = values
                parts[n, index] = values.astype(bf16)
        for k in range(1, groups):
            copy = remote(
                parts.at[n, group_at[k]], landed.at[k - 1, n], a_send.at[k - 1, n],
                a_recv.at[k - 1, n], (group_at[k], par),
            )
            copy.start()
            a_copies.append(copy)

    for copy in c_copies:
        copy.wait_recv()
    west_tile, east_tile, south_tile, north_tile = beside(par)
    west_rim, east_rim, south_rim, north_rim = (
        rims[index].astype(f32) for index in (west_tile, east_tile, south_tile, north_tile)
    )
    sums = around(
        own,
        chunks,
        lambda j: pltpu.roll(west_rim, LANES - chunks - j, 1),
        lambda j: pltpu.roll(east_rim, TSIDE - 1 - j, 1),
        jnp.where(lane < 16, pltpu.roll(south_rim, 48, 1), pltpu.roll(south_rim, 32, 1)),
        jnp.where(lane >= LANES - 16, pltpu.roll(north_rim, 64, 1), pltpu.roll(north_rim, 80, 1)),
    )
    for j in range(chunks):
        strength = coupling[:, j * LANES : (j + 1) * LANES]
        diagonal = kappa[:, j * LANES : (j + 1) * LANES] + 4.0 * strength
        at = slice(j * LANES % WIDE, j * LANES % WIDE + LANES)
        prior[j * LANES // WIDE, :, at] = diagonal * own[j] - strength * sums[j]

    def prepare(tile, carry):
        strength = couplings[tile]
        rate = 1.0 / (kappas[tile] + 4.0 * strength)
        start[tile] = jnp.broadcast_to(rate, (rows, cells))
        ratio[tile] = jnp.broadcast_to(strength * rate, (rows, cells))
        return carry

    lax.fori_loop(0, tiles, prepare, 0)
    even[tiles] = jnp.zeros((rows, cells), f32)
    odd[tiles] = jnp.zeros((rows, cells), f32)

    e_copies, b_copies = [], []
    for n in range(columns):
        total = misfit[n, sens] + prior[n]
        for k in range(1, groups):
            a_copies[n * (groups - 1) + k - 1].wait_recv()
            total = total + landed[k - 1, n].astype(f32)
        exact[n] = total.reshape(tiles, rows, WIDE)
        grad[n] = exact[n].astype(bf16)
        for q in range(1, tiles):
            copy = remote(
                exact.at[n, tile_at[q]], grad_in.at[par, n], b_send.at[n, q - 1],
                b_recv.at[n, q - 1], (sens, tile_at[q]),
            )
            copy.start()
            b_copies.append(copy)
        for k in range(1, groups):
            copy = remote(
                grad.at[n], grad_all.at[n, sens], e_send.at[n, k - 1], e_recv.at[n, k - 1],
                (group_at[k], par),
            )
            copy.start()
            e_copies.append(copy)
        grad_in[par, n] = exact[n, par]
        grad_all[n, sens] = grad[n]

    for copy in b_copies:
        copy.wait_recv()

    def begin(tile, carry):
        for n in range(columns):
            at = slice(n * WIDE, (n + 1) * WIDE)
            values = grad_in[tile, n] * start[tile, :, at]
            start[tile, :, at] = values
            even[tile, :, at] = values
        return carry

    lax.fori_loop(0, tiles, begin, 0)

    def relax(tile, old):
        west, east, south, north = beside(tile)

        def load(index, j):
            return old[index, :, j * LANES : (j + 1) * LANES]

        sums = around(
            [load(tile, j) for j in range(chunks)],
            chunks,
            lambda j: pltpu.roll(load(west, j), LANES - TSIDE + 1, 1),
            lambda j: pltpu.roll(load(east, j), TSIDE - 1, 1),
            pltpu.roll(load(south, chunks - 1), TSIDE, 1),
            pltpu.roll(load(north, 0), LANES - TSIDE, 1),
        )
        for j, total in enumerate(sums):
            at = slice(j * LANES, (j + 1) * LANES)
            yield at, start[tile, :, at] + ratio[tile, :, at] * total

    def sweep(count):
        old, new = (even, odd) if count % 2 == 0 else (odd, even)

        def one(tile, carry):
            for at, values in relax(tile, old):
                new[tile, :, at] = values
            return carry

        lax.fori_loop(0, tiles, one, 0, unroll=min(tiles, 8))

    for count in range(SWEEPS - 2):
        sweep(count)
    last = even if SWEEPS % 2 == 0 else odd
    d_copies = {}
    for q in far_first + [0]:
        for at, values in relax(tile_at[q], last):
            dir_send[tile_at[q], :, at] = values.astype(bf16)
        if q:
            copy = remote(
                dir_send.at[tile_at[q]], dir_all.at[sens, par], d_send.at[q - 1], d_recv.at[q - 1],
                (sens, tile_at[q]),
            )
            copy.start()
            d_copies[q] = copy
    dir_all[sens, par] = dir_send[par]
    f_copies = []

    def onward(q, group, targets):
        piece = dir_all.at[group, source_at[q]]
        out = []
        for k, target in targets:
            copy = remote(piece, piece, f_send.at[k, q], f_recv.at[k, q], (target, par))
            copy.start()
            out.append(copy)
        f_copies.extend(out)
        return out

    if groups == 4:
        beside_x, beside_y = sens + 1 - 2 * lax.rem(sens, 2), lax.rem(sens + 2, groups)
        direct, passed = {}, []

        def relay(index):
            q = near_first[index]
            origin, target = (beside_x, beside_y) if index % 2 == 0 else (beside_y, beside_x)
            direct[q][index % 2].wait_recv()
            passed.extend(onward(q, origin, [(2, target)]))

        lag = 2
        for index, q in enumerate(near_first):
            if q:
                d_copies[q].wait_recv()
            direct[q] = onward(q, sens, [(0, beside_x), (1, beside_y)])
            if index >= lag:
                relay(index - lag)
        for index in range(tiles - lag, tiles):
            relay(index)
        for index, q in enumerate(near_first):
            direct[q][1 - index % 2].wait_recv()
        for copy in passed:
            copy.wait_recv()
    else:
        for q in near_first:
            if q:
                d_copies[q].wait_recv()
            onward(q, sens, [(k - 1, group_at[k]) for k in range(1, groups)])
        for copy in f_copies:
            copy.wait_recv()
    for copy in e_copies:
        copy.wait_recv()
    d_copies = list(d_copies.values())
    for copy in p_copies + c_copies + a_copies + e_copies + b_copies + d_copies + f_copies:
        copy.wait_send()


def finish_kernel(stride, grad, direction, grad_out, dir_out):
    samples, count, rows, cells = direction.shape
    for b in range(samples):
        for i in range(count):
            for j in range(cells // LANES):
                to = pl.ds(i * rows * stride + samples * j + b, rows, stride=stride)
                at = slice(j * LANES, (j + 1) * LANES)
                n, inner = j * LANES // WIDE, slice(j * LANES % WIDE, j * LANES % WIDE + LANES)
                grad_out[to, :] = grad[n, b, i, :, inner].astype(f32)
                dir_out[to, :] = direction[b, i, :, at].astype(f32)


def per_device(
    kernel, param, observed, noise_scale, robust_flags, kappa_field, coupling, neighbours
):
    length, samples, cells = param.shape
    parts, count, sensors = kernel.shape[:3]
    groups, tiles = lax.axis_size("sens"), lax.axis_size("par")
    chunks, columns = cells // LANES, cells // WIDE
    freqs = -(-count // GROUP)
    span = length * samples // groups
    rows = span // tiles
    block = (rows, cells)
    raw = param.reshape(length, samples, chunks, LANES).transpose(0, 2, 1, 3)
    raw = raw.reshape(length * chunks * samples, LANES)
    consts = all_tables(length)
    vmem, smem = pl.BlockSpec(memory_space=pltpu.VMEM), pl.BlockSpec(memory_space=pltpu.SMEM)
    dma, scratch = pltpu.SemaphoreType.DMA, pltpu.VMEM
    hbm = pl.BlockSpec(memory_space=pl.ANY)
    sems = [
        (tiles - 1,), (tiles - 1,), (2, tiles - 1), (groups - 1, columns),
        (columns, groups - 1), (columns, tiles - 1), (tiles - 1,), (groups - 1, tiles),
    ]
    grad_all, dir_all = pl.pallas_call(
        functools.partial(main_kernel, groups, tiles),
        out_shape=(
            jax.ShapeDtypeStruct((columns, groups, tiles, rows, WIDE), bf16),
            jax.ShapeDtypeStruct((groups, tiles) + block, bf16),
        ),
        in_specs=[hbm] * 6 + [vmem] * 5 + [smem],
        out_specs=(vmem, vmem),
        scratch_shapes=[scratch(raw.shape, f32)]
        + [scratch(table.shape, bf16) for table in consts]
        + [
            scratch((freqs, parts, GROUP * sensors, cells), bf16),
            scratch((samples, 2 * length, cells), bf16),
            scratch((freqs, 2 * samples * GROUP, cells), bf16),
            scratch((freqs, HALF, LANES), f32),
            scratch((length, LANES), f32),
            scratch((length, LANES), f32),
            scratch((freqs, 2 * samples * GROUP, 2 * WIDE), bf16),
            scratch((samples, 3 * freqs * 2 * GROUP, WIDE), bf16),
            scratch((columns, groups, span, WIDE), f32),
            scratch((columns, groups, span, WIDE), bf16),
            scratch((groups - 1, columns, span, WIDE), bf16),
            scratch((columns, span, WIDE), f32),
            scratch((span, LANES), bf16),
            scratch((tiles + 1, span, LANES), bf16),
            scratch((tiles, 1, cells), f32),
            scratch((tiles, 1, cells), f32),
            scratch((columns, tiles, rows, WIDE), bf16),
            scratch((columns, tiles, rows, WIDE), f32),
            scratch((tiles, columns, rows, WIDE), f32),
            scratch((tiles,) + block, f32),
            scratch((tiles,) + block, f32),
            scratch((tiles + 1,) + block, f32),
            scratch((tiles + 1,) + block, f32),
            scratch((tiles,) + block, bf16),
            scratch((length // 4, LANES), f32),
            scratch((tiles - 1, length // 4, LANES), f32),
            dma((freqs, parts)),
            dma((5,)),
        ]
        + [dma(shape) for shape in sems for _ in range(2)],
        compiler_params=pltpu.CompilerParams(collective_id=0, has_side_effects=True),
    )(
        kernel.reshape(parts, count * sensors, cells), raw, *consts, observed, noise_scale[None],
        robust_flags, kappa_field[None], coupling[None], neighbours.T,
    )

    steps = max(1, length // rows // 2)
    each = length // rows // steps
    out = jax.ShapeDtypeStruct(raw.shape, f32)
    out_spec = pl.BlockSpec((raw.shape[0] // steps, LANES), lambda s: (s, 0))
    gradient, direction = pl.pallas_call(
        functools.partial(finish_kernel, chunks * samples),
        out_shape=(out, out),
        grid=(steps,),
        in_specs=[
            pl.BlockSpec((columns, samples, each, rows, WIDE), lambda s: (0, 0, s, 0, 0)),
            pl.BlockSpec((samples, each) + block, lambda s: (0, s, 0, 0)),
        ],
        out_specs=(out_spec, out_spec),
    )(
        grad_all.reshape(columns, samples, length // rows, rows, WIDE),
        dir_all.reshape((samples, length // rows) + block),
    )

    def restore(values):
        values = values.reshape(length, chunks, samples, LANES).transpose(0, 2, 1, 3)
        return values.reshape(param.shape)

    return restore(gradient), restore(direction)


def solution(mesh):
    return jax.shard_map(
        per_device,
        mesh=mesh,
        in_specs=(
            P(None, None, "sens", "par"),
            P(None, None, "par"),
            P("sens", None),
            P("sens"),
            P("sens", None),
            P("par"),
            P("par"),
            P(),
        ),
        out_specs=(P(None, None, "par"), P(None, None, "par")),
        check_vma=False,
    )
```

```python
import functools

import jax
import jax.numpy as jnp
import numpy as np
from jax import lax
from jax.experimental import pallas as pl
from jax.experimental.pallas import tpu as pltpu
from jax.sharding import PartitionSpec as P

SWEEPS = 8
TSIDE = 32
LANES = 128
GROUP = 16
HALF = 8
WIDE = 256

huber_limit = 1.345

MESH = pl.DeviceIdType.MESH
LAST = (((1,), (1,)), ((), ()))
f32, bf16 = jnp.float32, jnp.bfloat16


def tables(length):
    period = 2 * length
    frequency = np.arange(length + 1)
    phases = frequency[:, None] * np.arange(length)[None, :] % period
    angles = phases * (2.0 * np.pi / period)
    cosine, sines = np.cos(angles), np.sin(angles)
    forward = np.stack([cosine, -sines], 0)
    weight = np.where((frequency == 0) | (frequency == length), 1.0, 2.0) / period
    return forward, forward * weight[:, None]


def halves(table):
    high = table.astype(np.float32).astype(jnp.bfloat16)
    low = (table - high.astype(np.float64)).astype(np.float32).astype(jnp.bfloat16)
    return high, low


def pairs(table):
    high, low = halves(table)
    return np.concatenate(
        [np.concatenate([high, high], 1), np.concatenate([low, np.zeros_like(low)], 1)], 0
    )


def all_tables(length):
    forward, backward = tables(length)
    count = length + 1
    groups = -(-count // GROUP)
    full = count // GROUP
    pad = ((0, 0), (0, groups * GROUP - count), (0, 0))

    def rows(table):
        table = np.pad(table, pad).reshape(2, groups, GROUP, length)
        return table.transpose(1, 0, 2, 3).reshape(groups * 2 * GROUP, length)

    fore, back = rows(forward), rows(backward)
    trans = np.pad(backward, pad).reshape(2, groups, 2, HALF, length)
    trans = trans.transpose(0, 2, 4, 1, 3).reshape(4 * length, groups * HALF)
    high, low = (part.T for part in halves(fore))
    cut = full * 2 * GROUP
    main, rest = slice(0, cut), slice(cut, None)
    misfit = np.concatenate(
        [high[:, main], high[:, main], low[:, main], high[:, rest], high[:, rest], low[:, rest]], 1
    )

    def fill(table):
        return np.pad(table, ((0, 0), (0, -table.shape[1] % LANES)))

    return tuple(fill(table) for table in (pairs(fore), pairs(trans), pairs(back), misfit))


def split(values):
    high = values.astype(bf16)
    return high, (values - high.astype(f32)).astype(bf16)


def split_wide(values):
    high = values.astype(bf16).astype(f32)
    return high, values - high


def remote(src, dst, send, recv, device):
    return pltpu.make_async_remote_copy(
        src_ref=src, dst_ref=dst, send_sem=send, recv_sem=recv, device_id=device, device_id_type=MESH
    )


def around(own, chunks, west, east, south, north):
    shape = own[0].shape
    lane = lax.broadcasted_iota(jnp.int32, shape, 1)
    column = lax.rem(lane, TSIDE)
    up = [pltpu.roll(v, LANES - TSIDE, 1) for v in own] + [north]
    down = [south] + [pltpu.roll(v, TSIDE, 1) for v in own]
    sums = []
    for j in range(chunks):
        east_side = jnp.where(column == TSIDE - 1, east(j), pltpu.roll(own[j], LANES - 1, 1))
        west_side = jnp.where(column == 0, west(j), pltpu.roll(own[j], 1, 1))
        north_side = jnp.where(lane < LANES - TSIDE, up[j], up[j + 1])
        south_side = jnp.where(lane >= TSIDE, down[j + 1], down[j])
        sums.append((east_side + west_side) + (north_side + south_side))
    return sums


def main_kernel(
    groups, tiles,
    kernel, param_in, fore_in, trans_in, back_in, mist_in, observed, noise, flags, kappa, coupling, near,
    grad_all, dir_all,
    param, fore, trans, back, mist, blocks, halved, spectrum, packed, seen, bounded, wide, stacked,
    misfit, parts, landed, prior, rim, rims, kappas, couplings, grad, exact, grad_in, start, ratio,
    even, odd, dir_send, mine_out, others, k_sem, l_sem, k_send, k_recv, r_send, r_recv, c_send, c_recv,
    a_send, a_recv, e_send, e_recv, b_send, b_recv, d_send, d_recv, f_send, f_recv,
):
    sens, par = lax.axis_index("sens"), lax.axis_index("par")
    sensors, length = observed.shape
    freqs, pieces = spectrum.shape[0], blocks.shape[1]
    cells = halved.shape[2]
    samples = halved.shape[0]
    full = (length + 1) // GROUP
    chunks = cells // LANES
    columns = cells // WIDE
    stride = chunks * samples
    span = prior.shape[1]
    rows = span // tiles
    group_at = [lax.rem(sens + k, groups) for k in range(groups)]
    tile_at = [lax.rem(par + q, tiles) for q in range(tiles)]
    source_at = [lax.rem(par + tiles - q, tiles) for q in range(tiles)]

    barrier = pltpu.get_barrier_semaphore()
    for k in range(1, groups):
        pl.semaphore_signal(barrier, inc=1, device_id=(group_at[k], par), device_id_type=MESH)
    for q in range(1, tiles):
        pl.semaphore_signal(barrier, inc=1, device_id=(sens, tile_at[q]), device_id_type=MESH)

    early = [
        pltpu.make_async_copy(source, target, l_sem.at[index])
        for index, (source, target) in enumerate(
            [(param_in, param), (fore_in, fore), (trans_in, trans), (back_in, back), (mist_in, mist)]
        )
    ]

    def fetch(g, i, size):
        return pltpu.make_async_copy(
            kernel.at[i, pl.ds(g * GROUP * sensors, size)],
            blocks.at[g, i, pl.ds(0, size)],
            k_sem.at[g, i],
        )

    whole, rest = GROUP * sensors, (length + 1 - full * GROUP) * sensors
    for copy in early[:2]:
        copy.start()

    def begin_fetch(g, carry):
        for i in range(pieces):
            fetch(g, i, whole).start()
        return carry

    lax.fori_loop(0, full, begin_fetch, 0)
    for i in range(pieces):
        fetch(full, i, rest).start()
    for copy in early[2:]:
        copy.start()

    copies = LANES // sensors
    seen[...] = jnp.concatenate([observed[...]] * copies, 0).T
    bounded[...] = jnp.concatenate([flags[...].astype(f32)] * copies, 0).T
    deviation = jnp.concatenate([noise[...]] * copies, 1)
    inverse = 1.0 / deviation

    for copy in early[:2]:
        copy.wait()
    for b in range(samples):
        for j in range(chunks):
            high, low = split(param[pl.ds(samples * j + b, length, stride=stride), :])
            at = slice(j * LANES, (j + 1) * LANES)
            halved[b, :length, at] = high
            halved[b, length:, at] = low

    half = freqs * 2 * GROUP
    for b in range(samples):
        for n in range(columns):
            at = slice(n * WIDE, (n + 1) * WIDE)
            both = jnp.dot(fore[...], halved[b, :, at], preferred_element_type=f32)
            rounded = (both[:half] + both[half:]).astype(bf16)
            for g in range(freqs):
                for k in range(2):
                    to, fro = (k * samples + b) * GROUP, (g * 2 + k) * GROUP
                    spectrum[g, to : to + GROUP, at] = rounded[fro : fro + GROUP]

    lanes64 = lax.broadcasted_iota(jnp.int32, (2 * samples * GROUP, WIDE), 1) // sensors
    rows64 = lax.rem(lax.broadcasted_iota(jnp.int32, (2 * samples * GROUP, WIDE), 0), GROUP)
    keep = lanes64 == rows64
    place = lax.broadcasted_iota(jnp.int32, (HALF, LANES), 1) // sensors
    side = samples * GROUP

    def pack(real, imag):
        total = jnp.concatenate([real[:side] - imag[side:], real[side:] + imag[:side]], 0)
        for step in range(copies.bit_length() - 1):
            total = total + pltpu.roll(total, sensors << step, 1)
        out = jnp.zeros((HALF, LANES), f32)
        for r in range(copies):
            out = jnp.where(place == r, total[r * HALF : (r + 1) * HALF], out)
        return out

    for g in range(freqs):
        size = whole if g < full else rest
        for i in range(pieces):
            fetch(g, i, size).wait()
        folded = []
        for i in range(pieces):
            product = lax.dot_general(
                spectrum[g], blocks[g, i, :size], LAST, preferred_element_type=f32
            )
            if g < full:
                product = jnp.where(keep, product, 0.0)
                folded.append(product[:, :LANES] + product[:, LANES:])
            else:
                filler = jnp.zeros((product.shape[0], LANES - sensors), f32)
                folded.append(jnp.concatenate([product, filler], 1))
        packed[g] = pack(*folded)

    for copy in early[2:]:
        copy.wait()
    high, low = split_wide(packed[...].reshape(freqs * HALF, LANES))
    right = jnp.concatenate([high, low], 0).astype(bf16)
    both = jnp.dot(trans[:, : right.shape[0]], right, preferred_element_type=f32)
    both = both[: 4 * length] + both[4 * length :]

    def lane_group(count):
        where = lax.broadcasted_iota(jnp.int32, (count, LANES), 1) // sensors
        kind = where // (2 * samples) * 2 + lax.rem(where, 2)
        return lax.rem(where // 2, samples), kind

    kind = lane_group(length)[1]
    series = both[:length]
    for part in range(1, 4):
        series = jnp.where(kind == part, both[part * length : (part + 1) * length], series)
    series = series + jnp.where(
        lax.rem(kind, 2) == 0, pltpu.roll(series, LANES - sensors, 1), pltpu.roll(series, sensors, 1)
    )
    series = series + pltpu.roll(series, LANES // 2, 1)
    short = length // 4
    sample_of, kind = lane_group(short)
    share = series[:short]
    for part in range(1, 4):
        share = jnp.where(kind == part, series[part * short : (part + 1) * short], share)
    mine_out[...] = share

    others_at = list(range(1, tiles))
    pl.semaphore_wait(barrier, groups + tiles - 2)
    p_copies = []
    for q in others_at:
        copy = remote(
            mine_out, others.at[q - 1], k_send.at[q - 1], k_recv.at[q - 1], (sens, tile_at[q])
        )
        copy.start()
        p_copies.append(copy)

    first = sens * span
    own_sample, own_time = first // length, lax.rem(first, length)
    own = [
        param[pl.ds(own_time * stride + samples * j + own_sample, span, stride=stride), :]
        for j in range(chunks)
    ]
    lane = lax.broadcasted_iota(jnp.int32, (span, LANES), 1)
    column = lax.rem(lane, TSIDE)
    quarter = lane // TSIDE
    edge = jnp.zeros((span, LANES), f32)
    for j in range(chunks):
        edge = jnp.where(column == j, pltpu.roll(own[j], j, 1) if j else own[j], edge)
        shift = (chunks + j - (TSIDE - 1)) % LANES
        edge = jnp.where(column == chunks + j, pltpu.roll(own[j], shift, 1), edge)
    upper = column >= TSIDE // 2
    edge = jnp.where(upper & (quarter == 0), pltpu.roll(own[0], 16, 1), edge)
    edge = jnp.where(upper & (quarter == 1), pltpu.roll(own[0], 32, 1), edge)
    edge = jnp.where(upper & (quarter == 2), pltpu.roll(own[-1], LANES - 16, 1), edge)
    edge = jnp.where(upper & (quarter == 3), own[-1], edge)
    rim[...] = edge.astype(bf16)
    c_copies = []
    for q in range(1, tiles):
        device = (sens, tile_at[q])
        c_copies.append(remote(rim, rims.at[par], r_send.at[q - 1], r_recv.at[q - 1], device))
        c_copies.append(
            remote(kappa, kappas.at[par], c_send.at[0, q - 1], c_recv.at[0, q - 1], device)
        )
        c_copies.append(
            remote(coupling, couplings.at[par], c_send.at[1, q - 1], c_recv.at[1, q - 1], device)
        )
    for copy in c_copies:
        copy.start()
    rims[tiles] = jnp.zeros((span, LANES), bf16)
    kappas[par] = kappa[...]
    couplings[par] = coupling[...]

    def beside(tile):
        return [jnp.where(near[s, tile] < 0, tiles, near[s, tile]) for s in range(4)]

    for copy in p_copies:
        copy.wait_recv()
    total = mine_out[...]
    for q in range(tiles - 1):
        total = total + others[q]
    adjoint = []
    for b in range(samples):
        mine = jnp.concatenate(
            [jnp.where((sample_of == b) & (kind == part), total, 0.0) for part in range(4)], 0
        )
        for step in range(copies.bit_length() - 1):
            mine = mine + pltpu.roll(mine, sensors << step, 1)
        scaled = (mine - seen[...]) * inverse
        robust = jnp.where(bounded[...] == 1.0, jnp.clip(scaled, -huber_limit, huber_limit), scaled)
        high, low = split(robust * inverse)
        both = jnp.dot(back[...], jnp.concatenate([high, low], 0), preferred_element_type=f32)
        adjoint.append(both[:half] + both[half:])
    own_row = lax.broadcasted_iota(jnp.int32, (HALF, LANES), 0)
    blank = jnp.zeros((HALF, LANES), f32)
    for g in range(freqs):
        for k in range(2):
            for b in range(samples):
                fro = (g * 2 + k) * GROUP
                piece = adjoint[b][fro : fro + GROUP]
                pick = [
                    jnp.where(own_row == place, piece[h * HALF : (h + 1) * HALF], 0.0)
                    for h in range(2)
                ]
                here = [
                    jnp.concatenate([pick[0], blank], 0), jnp.concatenate([blank, pick[1]], 0)
                ]
                to = (k * samples + b) * GROUP
                other = ((1 - k) * samples + b) * GROUP
                for h in range(2):
                    at = slice(h * LANES, (h + 1) * LANES)
                    wide[g, to : to + GROUP, at] = here[h].astype(bf16)
                    at = slice(WIDE + h * LANES, WIDE + (h + 1) * LANES)
                    turned = here[h] if k else -here[h]
                    wide[g, other : other + GROUP, at] = turned.astype(bf16)

    deep = full * 2 * GROUP
    a_copies = []
    for n in range(columns):
        at = slice(n * WIDE, (n + 1) * WIDE)
        for g in range(freqs):
            if g < full:
                product = jnp.dot(
                    wide[g], blocks[g, :, :, at].reshape(2 * WIDE, WIDE), preferred_element_type=f32
                )
            else:
                product = jnp.dot(
                    wide[g, :, :sensors], blocks[g, 0, :sensors, at], preferred_element_type=f32
                ) + jnp.dot(
                    wide[g, :, WIDE : WIDE + sensors], blocks[g, 1, :sensors, at],
                    preferred_element_type=f32,
                )
            high, low = split(product)
            for k in range(2):
                for b in range(samples):
                    fro = (k * samples + b) * GROUP
                    if g < full:
                        base, gap = (g * 2 + k) * GROUP, deep
                    else:
                        base, gap = 3 * deep + k * GROUP, 2 * GROUP
                    stacked[b, base : base + GROUP] = high[fro : fro + GROUP]
                    stacked[b, base + gap : base + gap + GROUP] = low[fro : fro + GROUP]
                    stacked[b, base + 2 * gap : base + 2 * gap + GROUP] = high[fro : fro + GROUP]
        for b in range(samples):
            result = jnp.dot(mist[:, : stacked.shape[1]], stacked[b], preferred_element_type=f32)
            for piece in range(length // span):
                index = b * (length // span) + piece
                values = result[piece * span : (piece + 1) * span]
                misfit[n, index] = values
                parts[n, index] = values.astype(bf16)
        for k in range(1, groups):
            copy = remote(
                parts.at[n, group_at[k]], landed.at[k - 1, n], a_send.at[k - 1, n],
                a_recv.at[k - 1, n], (group_at[k], par),
            )
            copy.start()
            a_copies.append(copy)

    for copy in c_copies:
        copy.wait_recv()
    west_tile, east_tile, south_tile, north_tile = beside(par)
    west_rim, east_rim, south_rim, north_rim = (
        rims[index].astype(f32) for index in (west_tile, east_tile, south_tile, north_tile)
    )
    sums = around(
        own,
        chunks,
        lambda j: pltpu.roll(west_rim, LANES - chunks - j, 1),
        lambda j: pltpu.roll(east_rim, TSIDE - 1 - j, 1),
        jnp.where(lane < 16, pltpu.roll(south_rim, 48, 1), pltpu.roll(south_rim, 32, 1)),
        jnp.where(lane >= LANES - 16, pltpu.roll(north_rim, 64, 1), pltpu.roll(north_rim, 80, 1)),
    )
    for j in range(chunks):
        strength = coupling[:, j * LANES : (j + 1) * LANES]
        diagonal = kappa[:, j * LANES : (j + 1) * LANES] + 4.0 * strength
        at = slice(j * LANES % WIDE, j * LANES % WIDE + LANES)
        prior[j * LANES // WIDE, :, at] = diagonal * own[j] - strength * sums[j]

    def prepare(tile, carry):
        strength = couplings[tile]
        rate = 1.0 / (kappas[tile] + 4.0 * strength)
        start[tile] = jnp.broadcast_to(rate, (rows, cells))
        ratio[tile] = jnp.broadcast_to(strength * rate, (rows, cells))
        return carry

    lax.fori_loop(0, tiles, prepare, 0)
    even[tiles] = jnp.zeros((rows, cells), f32)
    odd[tiles] = jnp.zeros((rows, cells), f32)

    e_copies, b_copies = [], []
    for n in range(columns):
        total = misfit[n, sens] + prior[n]
        for k in range(1, groups):
            a_copies[n * (groups - 1) + k - 1].wait_recv()
            total = total + landed[k - 1, n].astype(f32)
        exact[n] = total.reshape(tiles, rows, WIDE)
        grad[n] = exact[n].astype(bf16)
        for q in range(1, tiles):
            copy = remote(
                exact.at[n, tile_at[q]], grad_in.at[par, n], b_send.at[n, q - 1],
                b_recv.at[n, q - 1], (sens, tile_at[q]),
            )
            copy.start()
            b_copies.append(copy)
        for k in range(1, groups):
            copy = remote(
                grad.at[n], grad_all.at[n, sens], e_send.at[n, k - 1], e_recv.at[n, k - 1],
                (group_at[k], par),
            )
            copy.start()
            e_copies.append(copy)
        grad_in[par, n] = exact[n, par]
        grad_all[n, sens] = grad[n]

    for copy in b_copies:
        copy.wait_recv()

    def begin(tile, carry):
        for n in range(columns):
            at = slice(n * WIDE, (n + 1) * WIDE)
            values = grad_in[tile, n] * start[tile, :, at]
            start[tile, :, at] = values
            even[tile, :, at] = values
        return carry

    lax.fori_loop(0, tiles, begin, 0)

    def relax(tile, old):
        west, east, south, north = beside(tile)

        def load(index, j):
            return old[index, :, j * LANES : (j + 1) * LANES]

        sums = around(
            [load(tile, j) for j in range(chunks)],
            chunks,
            lambda j: pltpu.roll(load(west, j), LANES - TSIDE + 1, 1),
            lambda j: pltpu.roll(load(east, j), TSIDE - 1, 1),
            pltpu.roll(load(south, chunks - 1), TSIDE, 1),
            pltpu.roll(load(north, 0), LANES - TSIDE, 1),
        )
        for j, total in enumerate(sums):
            at = slice(j * LANES, (j + 1) * LANES)
            yield at, start[tile, :, at] + ratio[tile, :, at] * total

    def sweep(count):
        old, new = (even, odd) if count % 2 == 0 else (odd, even)

        def one(tile, carry):
            for at, values in relax(tile, old):
                new[tile, :, at] = values
            return carry

        lax.fori_loop(0, tiles, one, 0, unroll=min(tiles, 8))

    for count in range(SWEEPS - 2):
        sweep(count)
    last = even if SWEEPS % 2 == 0 else odd
    d_copies = {}
    for q in others_at + [0]:
        for at, values in relax(tile_at[q], last):
            dir_send[tile_at[q], :, at] = values.astype(bf16)
        if q:
            copy = remote(
                dir_send.at[tile_at[q]], dir_all.at[sens, par], d_send.at[q - 1], d_recv.at[q - 1],
                (sens, tile_at[q]),
            )
            copy.start()
            d_copies[q] = copy
    dir_all[sens, par] = dir_send[par]
    f_copies = []

    for q in range(tiles):
        if q:
            d_copies[q].wait_recv()
        piece = dir_all.at[sens, source_at[q]]
        for k in range(1, groups):
            copy = remote(
                piece, piece, f_send.at[k - 1, q], f_recv.at[k - 1, q], (group_at[k], par)
            )
            copy.start()
            f_copies.append(copy)
    for copy in f_copies:
        copy.wait_recv()
    for copy in e_copies:
        copy.wait_recv()
    d_copies = list(d_copies.values())
    for copy in p_copies + c_copies + a_copies + e_copies + b_copies + d_copies + f_copies:
        copy.wait_send()


def finish_kernel(stride, grad, direction, grad_out, dir_out):
    samples, count, rows, cells = direction.shape
    for b in range(samples):
        for i in range(count):
            for j in range(cells // LANES):
                to = pl.ds(i * rows * stride + samples * j + b, rows, stride=stride)
                at = slice(j * LANES, (j + 1) * LANES)
                n, inner = j * LANES // WIDE, slice(j * LANES % WIDE, j * LANES % WIDE + LANES)
                grad_out[to, :] = grad[n, b, i, :, inner].astype(f32)
                dir_out[to, :] = direction[b, i, :, at].astype(f32)


def per_device(
    kernel, param, observed, noise_scale, robust_flags, kappa_field, coupling, neighbours
):
    length, samples, cells = param.shape
    parts, count, sensors = kernel.shape[:3]
    groups, tiles = lax.axis_size("sens"), lax.axis_size("par")
    chunks, columns = cells // LANES, cells // WIDE
    freqs = -(-count // GROUP)
    span = length * samples // groups
    rows = span // tiles
    block = (rows, cells)
    raw = param.reshape(length, samples, chunks, LANES).transpose(0, 2, 1, 3)
    raw = raw.reshape(length * chunks * samples, LANES)
    consts = all_tables(length)
    vmem, smem = pl.BlockSpec(memory_space=pltpu.VMEM), pl.BlockSpec(memory_space=pltpu.SMEM)
    dma, scratch = pltpu.SemaphoreType.DMA, pltpu.VMEM
    hbm = pl.BlockSpec(memory_space=pl.ANY)
    sems = [
        (tiles - 1,), (tiles - 1,), (2, tiles - 1), (groups - 1, columns),
        (columns, groups - 1), (columns, tiles - 1), (tiles - 1,), (groups - 1, tiles),
    ]
    grad_all, dir_all = pl.pallas_call(
        functools.partial(main_kernel, groups, tiles),
        out_shape=(
            jax.ShapeDtypeStruct((columns, groups, tiles, rows, WIDE), bf16),
            jax.ShapeDtypeStruct((groups, tiles) + block, bf16),
        ),
        in_specs=[hbm] * 6 + [vmem] * 5 + [smem],
        out_specs=(vmem, vmem),
        scratch_shapes=[scratch(raw.shape, f32)]
        + [scratch(table.shape, bf16) for table in consts]
        + [
            scratch((freqs, parts, GROUP * sensors, cells), bf16),
            scratch((samples, 2 * length, cells), bf16),
            scratch((freqs, 2 * samples * GROUP, cells), bf16),
            scratch((freqs, HALF, LANES), f32),
            scratch((length, LANES), f32),
            scratch((length, LANES), f32),
            scratch((freqs, 2 * samples * GROUP, 2 * WIDE), bf16),
            scratch((samples, 3 * freqs * 2 * GROUP, WIDE), bf16),
            scratch((columns, groups, span, WIDE), f32),
            scratch((columns, groups, span, WIDE), bf16),
            scratch((groups - 1, columns, span, WIDE), bf16),
            scratch((columns, span, WIDE), f32),
            scratch((span, LANES), bf16),
            scratch((tiles + 1, span, LANES), bf16),
            scratch((tiles, 1, cells), f32),
            scratch((tiles, 1, cells), f32),
            scratch((columns, tiles, rows, WIDE), bf16),
            scratch((columns, tiles, rows, WIDE), f32),
            scratch((tiles, columns, rows, WIDE), f32),
            scratch((tiles,) + block, f32),
            scratch((tiles,) + block, f32),
            scratch((tiles + 1,) + block, f32),
            scratch((tiles + 1,) + block, f32),
            scratch((tiles,) + block, bf16),
            scratch((length // 4, LANES), f32),
            scratch((tiles - 1, length // 4, LANES), f32),
            dma((freqs, parts)),
            dma((5,)),
        ]
        + [dma(shape) for shape in sems for _ in range(2)],
        compiler_params=pltpu.CompilerParams(collective_id=0, has_side_effects=True),
    )(
        kernel.reshape(parts, count * sensors, cells), raw, *consts, observed, noise_scale[None],
        robust_flags, kappa_field[None], coupling[None], neighbours.T,
    )

    steps = 2
    each = length // rows // steps
    out = jax.ShapeDtypeStruct(raw.shape, f32)
    out_spec = pl.BlockSpec((raw.shape[0] // steps, LANES), lambda s: (s, 0))
    gradient, direction = pl.pallas_call(
        functools.partial(finish_kernel, chunks * samples),
        out_shape=(out, out),
        grid=(steps,),
        in_specs=[
            pl.BlockSpec((columns, samples, each, rows, WIDE), lambda s: (0, 0, s, 0, 0)),
            pl.BlockSpec((samples, each) + block, lambda s: (0, s, 0, 0)),
        ],
        out_specs=(out_spec, out_spec),
    )(
        grad_all.reshape(columns, samples, length // rows, rows, WIDE),
        dir_all.reshape((samples, length // rows) + block),
    )

    def restore(values):
        values = values.reshape(length, chunks, samples, LANES).transpose(0, 2, 1, 3)
        return values.reshape(param.shape)

    return restore(gradient), restore(direction)


def solution(mesh):
    return jax.shard_map(
        per_device,
        mesh=mesh,
        in_specs=(
            P(None, None, "sens", "par"),
            P(None, None, "par"),
            P("sens", None),
            P("sens"),
            P("sens", None),
            P("par"),
            P("par"),
            P(),
        ),
        out_specs=(P(None, None, "par"), P(None, None, "par")),
        check_vma=False,
    )
```
